32 devices in a mesh: dp: 16 (over z, y, x), mp: 2 (over core).
Axes of the slice: x: 2, y: 2, z: 4, core: 2. Of those that a mesh axis runs over, the one named last changes fastest.
Arguments:
- hot_rows: int32 [16, 16, 32], P('dp'), may hold values from 0 to 4095
- hot_count: int32 [16, 16], P('dp'), may hold values from 1 to 32, as said below
- hot_cot: bfloat16 [16, 16, 32, 128], P('dp'), may hold values from -6 to 6
- table: float32 [65536, 128], P('dp'), may hold values from -3 to 3
- cold_ids: int32 [16384], P('dp'), may hold values from 0 to 1048575
- hash_mult: int32 [1024], replicated, may hold values from 1 to 1023
- hash_add: int32 [1024], replicated, may hold values from 0 to 1000002
- layer_one: bfloat16 [1024, 1024], P(None, 'mp'), may hold values from -0.1875 to 0.1875
- layer_two: bfloat16 [1024, 1024], P('mp'), may hold values from -0.1875 to 0.1875
- layer_three: bfloat16 [1024, 1024], P(None, 'mp'), may hold values from -0.1875 to 0.1875
- layer_four: bfloat16 [1024, 128], P('mp'), may hold values from -0.1875 to 0.1875
- cold_cot: bfloat16 [16384, 128], P('dp'), may hold values from -6 to 6
Outputs:
- hot_emb: bfloat16 [16, 16, 32, 128], P('dp')
- new_table: float32 [65536, 128], P('dp')
- cold_emb: bfloat16 [16384, 128], P('dp')
- grad_one: float32 [1024, 1024], P(None, 'mp')
- grad_two: float32 [1024, 1024], P('mp')
- grad_three: float32 [1024, 1024], P(None, 'mp')
- grad_four: float32 [1024, 128], P('mp')
The draws below stay inside these ranges and needn't reach their ends.
Inputs may be any that keep to these rules, and one draw needn't show every extreme that they name: `hot_rows`: entries index the owner's block of 4096 rows; entries in unused slots are arbitrary. `hot_count`: every batch shard fills all 32 slots of some owner, and some owner receives 32 from every batch shard.
All inputs are finite; a program needn't handle non-finite values.
Results may differ from the reference program's by a relative error of at most 0.0074.
Values may be sent and summed in bfloat16 or wider, within the bound.
No kernel may reach another device: no remote copies, remote signals or barrier semaphores. Data moves between devices by JAX's collectives and lax.ppermute only.
A program may use at most 128 MiB of HBM per device.

```python
import jax
import jax.numpy as jnp

E = 128
F = 1024
H = 1024
HOT_DEV = 4096
CAP = 32
HOT = 65536
COLDS = 16384
N_DP = 16


def draw_hot_count(key, part):
    first = jax.random.fold_in(key, 11)
    second = jax.random.fold_in(key, 12)
    third = jax.random.fold_in(key, 13)
    counts = jax.random.randint(first, (N_DP, N_DP), 1, CAP + 1)
    own_full = jax.random.randint(second, (N_DP, 1), 0, N_DP)
    common = jax.random.randint(third, (), 0, N_DP)
    columns = jnp.arange(N_DP)[None, :]
    filled = (columns == own_full) | (columns == common)
    return jnp.where(filled, CAP, counts).astype(jnp.int32)


def place_ends(entries, own_key, least, top_value):
    longest = entries.shape.index(max(entries.shape))
    spots = []
    for shift in (0, 1):
        where = [jax.random.randint(jax.random.fold_in(own_key, axis), (), 0, length) for axis, length in enumerate(entries.shape)]
        where[longest] = (where[longest] + shift) % entries.shape[longest]
        spots.append(tuple(where))
    return entries.at[spots[0]].set(least).at[spots[1]].set(top_value)


def shard_levels(rng, shape, cuts, smallest, top_value):
    loudness, own = 1.0, jax.random.fold_in(rng, 6)
    for position, shards_of in cuts:
        steps = jnp.exp(jax.random.uniform(jax.random.fold_in(own, position), (shards_of,), jnp.float32, smallest / len(cuts), top_value / len(cuts)))
        loudness = loudness * jnp.repeat(steps, shape[position] // shards_of).reshape([-1 if axis == position else 1 for axis in range(len(shape))])
    return loudness


def scatter_about(stream_key, shape, deviation, limit, shards=(), kind=jnp.bfloat16):
    values = deviation * jax.random.normal(stream_key, shape, jnp.float32)
    if shards:
        values = values * shard_levels(stream_key, shape, shards, -0.22, 0.18)
    return jnp.clip(values, -limit, limit).astype(kind)


def setup_inputs(seed: int = 0) -> dict:
    arg_keys = jax.random.split(jax.random.key(seed), 13)
    hot_rows = place_ends(jax.random.randint(arg_keys[0], (N_DP, N_DP, CAP), 0, HOT_DEV), jax.random.fold_in(arg_keys[0], 1), 0, HOT_DEV - 1).astype(jnp.int32)
    hot_count = draw_hot_count(jax.random.fold_in(arg_keys[12], 71), 0)
    hot_cot = scatter_about(arg_keys[2], (N_DP, N_DP, CAP, E), 1.0, 6.0, ((0, 16),))
    table = scatter_about(arg_keys[3], (HOT, E), 0.5, 3.0, ((0, 16),), jnp.float32)
    cold_ids = place_ends(jax.random.randint(arg_keys[4], (COLDS,), 0, 1048576), jax.random.fold_in(arg_keys[4], 1), 0, 1048575).astype(jnp.int32)
    hash_mult = place_ends(jax.random.randint(arg_keys[5], (F,), 1, 1024), jax.random.fold_in(arg_keys[5], 1), 1, 1023).astype(jnp.int32)
    hash_add = place_ends(jax.random.randint(arg_keys[6], (F,), 0, 1000003), jax.random.fold_in(arg_keys[6], 1), 0, 1000002).astype(jnp.int32)
    layer_one = scatter_about(arg_keys[7], (F, H), F ** -0.5, 0.1875, ((1, 2),))
    layer_two = scatter_about(arg_keys[8], (H, H), H ** -0.5, 0.1875, ((0, 2),))
    layer_three = scatter_about(arg_keys[9], (H, H), H ** -0.5, 0.1875, ((1, 2),))
    layer_four = scatter_about(arg_keys[10], (H, E), H ** -0.5, 0.1875, ((0, 2),))
    cold_cot = scatter_about(arg_keys[11], (COLDS, E), 1.0, 6.0, ((0, 16),))
    return dict(hot_rows=hot_rows, hot_count=hot_count, hot_cot=hot_cot, table=table, cold_ids=cold_ids, hash_mult=hash_mult, hash_add=hash_add, layer_one=layer_one, layer_two=layer_two, layer_three=layer_three, layer_four=layer_four, cold_cot=cold_cot)


learn_rate = 0.5
modulus = 1000003

def features_of(ids, hash_mult, hash_add):
    hashed = jnp.remainder(ids[:, None] * hash_mult[None, :] + hash_add[None, :], modulus)
    return (hashed.astype(jnp.float32) * (2.0 / 1000002.0) - 1.0).astype(jnp.bfloat16)

def silu_grad(value):
    sig = jax.nn.sigmoid(value)
    return sig * (1.0 + value * (1.0 - sig))

def reference(hot_rows, hot_count, hot_cot, table, cold_ids, hash_mult, hash_add, layer_one, layer_two, layer_three, layer_four, cold_cot):
    slots = jnp.arange(CAP, dtype=jnp.int32)
    used = slots[None, None, :] < hot_count[:, :, None]
    owners = jnp.arange(N_DP, dtype=jnp.int32)[None, :, None] * HOT_DEV
    row = (owners + hot_rows).astype(jnp.int32)
    hot_emb = jnp.where(used[..., None], table[row], 0.0).astype(jnp.bfloat16)
    masked = jnp.where(used[..., None], hot_cot.astype(jnp.float32), 0.0)
    table_grad = jnp.zeros_like(table).at[row.reshape(-1)].add(masked.reshape(-1, E))
    new_table = table - learn_rate * table_grad
    feats = features_of(cold_ids, hash_mult, hash_add)
    pre_one = jnp.dot(feats, layer_one, preferred_element_type=jnp.float32)
    act_one = jax.nn.silu(pre_one).astype(jnp.bfloat16)
    pre_two = jnp.dot(act_one, layer_two, preferred_element_type=jnp.float32)
    act_two = jax.nn.silu(pre_two).astype(jnp.bfloat16)
    pre_three = jnp.dot(act_two, layer_three, preferred_element_type=jnp.float32)
    act_three = jax.nn.silu(pre_three).astype(jnp.bfloat16)
    cold_emb = jnp.dot(act_three, layer_four, preferred_element_type=jnp.float32).astype(jnp.bfloat16)
    back_three = (jnp.dot(cold_cot, layer_four.T, preferred_element_type=jnp.float32) * silu_grad(pre_three)).astype(jnp.bfloat16)
    back_two = (jnp.dot(back_three, layer_three.T, preferred_element_type=jnp.float32) * silu_grad(pre_two)).astype(jnp.bfloat16)
    back_one = (jnp.dot(back_two, layer_two.T, preferred_element_type=jnp.float32) * silu_grad(pre_one)).astype(jnp.bfloat16)
    factor = float(COLDS) ** (-0.5)
    grad_four = jnp.dot(act_three.T, cold_cot, preferred_element_type=jnp.float32) * factor
    grad_three = jnp.dot(act_two.T, back_three, preferred_element_type=jnp.float32) * factor
    grad_two = jnp.dot(act_one.T, back_two, preferred_element_type=jnp.float32) * factor
    grad_one = jnp.dot(feats.T, back_one, preferred_element_type=jnp.float32) * factor
    return (hot_emb, new_table, cold_emb, grad_one, grad_two, grad_three, grad_four)
```

```python
import functools

import jax
import jax.numpy as jnp
from jax import lax
from jax.experimental import pallas as pl
from jax.experimental.pallas import tpu as pltpu
from jax.sharding import PartitionSpec as P


learn_rate = 0.5
modulus = 1000003
BF = jnp.bfloat16
F32 = jnp.float32


def hops_of(mesh):
    count = mesh.shape["dp"]
    coords = [getattr(d, "coords", None) for d in mesh.devices[:, 0]]
    sizes = None
    if all(c is not None for c in coords):
        sizes = [len({c[axis] for c in coords}) for axis in range(3)]
        if sizes[0] * sizes[1] * sizes[2] != count:
            sizes = None
    if sizes is None:
        sizes = [2] * (count.bit_length() - 1)
    hops, base = [], 0
    for size in sizes:
        bits = size.bit_length() - 1
        assert size == 1 << bits
        if bits == 2:
            hops.append([(1 << base, 3 << base), (3 << base, 2 << base)])
        elif bits:
            hops.append([(1 << (base + k), 1 << (base + k)) for k in range(bits)])
        base += bits
    assert 1 << base == count
    flat = []
    while any(hops):
        for group in hops:
            if group:
                flat.append(group.pop(0))
    return flat


TILE = 512


def dot(a, b):
    return jnp.dot(a, b, preferred_element_type=F32)


def dot_t(a, b):
    return lax.dot_general(a, b, (((0,), (0,)), ((), ())), preferred_element_type=F32)


def dot_bt(a, b):
    return lax.dot_general(a, b, (((1,), (1,)), ((), ())), preferred_element_type=F32)


def gates(value):
    sig = jax.nn.sigmoid(value)
    return (value * sig).astype(BF), sig * (1.0 + value * (1.0 - sig))


def tiles(size, body):
    step = min(size, TILE)

    def run(j, carry):
        body(pl.ds(pl.multiple_of(j * step, step), step))
        return carry

    lax.fori_loop(0, size // step, run, 0)


class Refs:
    def __init__(self, inputs, outputs, held, kept, load_sems, store_sems):
        self.held, self.kept = held, kept
        self.loads = [pltpu.make_async_copy(s, d, load_sems.at[i]) for i, (s, d) in enumerate(zip(inputs, held))]
        self.stores = [pltpu.make_async_copy(s, d, store_sems.at[i]) for i, (s, d) in enumerate(zip(kept, outputs))]
        self.waited, self.put = set(), set()
        for load in self.loads:
            load.start()

    def need(self, *which):
        for i in which:
            if i not in self.waited:
                self.loads[i].wait()
                self.waited.add(i)
        return tuple(self.held[i] for i in which)

    def store(self, *which):
        for i in which:
            self.stores[i].start()
            self.put.add(i)

    def finish(self):
        self.need(*range(len(self.loads)))
        self.store(*(i for i in range(len(self.stores)) if i not in self.put))
        for copy in self.stores:
            copy.wait()


def call(kernel, outs, args, scratch=(), flops=0, scalars=(), shared=()):
    shapes = [jax.ShapeDtypeStruct(shape, kind) for shape, kind in outs]
    moved = sum(x.size * x.dtype.itemsize for x in list(args) + shapes)
    far = pl.BlockSpec(memory_space=pltpu.MemorySpace.HBM)
    near = pl.BlockSpec(memory_space=pltpu.SMEM)
    p, n, m = len(scalars), len(args), len(shapes)
    shared = dict(shared)
    alone = [i for i in range(n) if i not in shared]
    scalars = [jnp.asarray(x, jnp.int32).reshape(-1) for x in scalars]

    def body(*refs):
        numbers, refs = refs[:p], refs[p:]
        inputs, outputs, refs = refs[:n], refs[n : n + m], refs[n + m :]
        own, kept, rest = refs[: len(alone)], refs[len(alone) : len(alone) + m], refs[len(alone) + m :]
        own = dict(zip(alone, own))
        held = [own[i] if i in own else kept[shared[i]] for i in range(n)]
        r = Refs(inputs, outputs, held, kept, rest[-2], rest[-1])
        kernel(r, *numbers, *rest[:-2])
        r.finish()

    return pl.pallas_call(
        body,
        out_shape=shapes,
        in_specs=[near] * p + [far] * n,
        out_specs=[far] * m,
        scratch_shapes=[
            *(pltpu.VMEM(args[i].shape, args[i].dtype) for i in alone),
            *(pltpu.VMEM(x.shape, x.dtype) for x in shapes),
            *(pltpu.VMEM(shape, kind) for shape, kind in scratch),
            pltpu.SemaphoreType.DMA((n,)),
            pltpu.SemaphoreType.DMA((m,)),
        ],
        cost_estimate=pl.CostEstimate(flops=flops, bytes_accessed=moved, transcendentals=0),
    )(*scalars, *args)


def first_kernel(r, core):
    ids, mult, add = r.need(0, 1, 2)
    feats, act, slope = r.kept
    rows = feats.shape[0]
    step = min(rows, 64)

    def hash_rows(j, carry):
        at = pl.ds(pl.multiple_of(j * step, step), step)
        own = pl.ds(pl.multiple_of(core[0] * rows + j * step, step), step)
        hashed = ids[own, :] * mult[...] + add[...]
        quotient = (hashed.astype(F32) * (1.0 / modulus)).astype(jnp.int32)
        left = hashed - quotient * modulus
        left = jnp.where(left < 0, left + modulus, left)
        left = jnp.where(left >= modulus, left - modulus, left)
        feats[at, :] = (left.astype(F32) * (2.0 / 1000002.0) - 1.0).astype(BF)
        return carry

    lax.fori_loop(0, rows // step, hash_rows, 0)
    r.store(0)
    (one,) = r.need(3)

    def layer(at):
        act[:, at], slope[:, at] = gates(dot(feats[...], one[:, at]))

    tiles(one.shape[1], layer)


def second_kernel(r, core, slope_three_m, slope_three_o):
    act_o, slope_one_o, act_two, slope_two, emb, back_m, back_o, act_three_m, act_three_o = r.kept
    feats, one_o = r.need(0, 1)

    def layer_one(at):
        act_o[:, at], slope_one_o[:, at] = gates(dot(feats[...], one_o[:, at]))

    tiles(one_o.shape[1], layer_one)
    r.store(0, 1)
    act_m, two_m, two_o = r.need(2, 3, 4)

    def layer_two(at):
        act_two[:, at], slope_two[:, at] = gates(
            dot(act_m[...], two_m[:, at]) + dot(act_o[...], two_o[:, at])
        )

    tiles(two_m.shape[1], layer_two)
    r.store(2, 3)
    three_m, three_o, four_m, four_o, cots = r.need(5, 6, 7, 8, 9)
    rows = act_two.shape[0]
    cot = cots.at[pl.ds(pl.multiple_of(core[0] * rows, rows), rows), :]
    for three, four, act, slope, back, places in (
        (three_o, four_o, act_three_o, slope_three_o, back_o, (8, 6)),
        (three_m, four_m, act_three_m, slope_three_m, back_m, (7, 5)),
    ):

        def layer_three(at):
            act[:, at], slope[:, at] = gates(dot(act_two[...], three[:, at]))
            back[:, at] = (dot_bt(cot[...], four[at, :]) * slope[:, at]).astype(BF)

        tiles(three.shape[1], layer_three)
        r.store(*places)
    emb[...] = (dot(act_three_m[...], four_m[...]) + dot(act_three_o[...], four_o[...])).astype(BF)


def back_kernel(r):
    back_two, back_one_m, back_one_o = r.kept
    back_m, back_o, three_m, three_o, slope_two = r.need(0, 1, 2, 3, 4)

    def go_back(at):
        back_two[:, at] = (
            (dot_bt(back_m[...], three_m[at, :]) + dot_bt(back_o[...], three_o[at, :])) * slope_two[:, at]
        ).astype(BF)

    tiles(three_m.shape[0], go_back)
    r.store(0)
    two_o, slope_o, two_m, slope_m = r.need(5, 6, 7, 8)
    for two, slope, back, place in ((two_o, slope_o, back_one_o, 2), (two_m, slope_m, back_one_m, 1)):

        def go_back(at):
            back[:, at] = (dot_bt(back_two[...], two[at, :]) * slope[:, at]).astype(BF)

        tiles(two.shape[0], go_back)
        r.store(place)


def grad_kernel(r, bit):
    left, left_o, right, right_o = r.need(0, 1, 2, 3)
    half = r.kept[0].shape[0]
    for place, of in ((0, 1 - bit[0]), (1, bit[0])):
        out = r.kept[place]

        def grads(at):
            rows = pl.ds(pl.multiple_of(of * half + at.start, min(half, TILE)), at.size)
            out[at, :] = (dot_t(left[:, rows], right[...]) + dot_t(left_o[:, rows], right_o[...])).astype(BF)

        tiles(half, grads)
        r.store(place)


def grads_kernel(r, bit, core):
    left, left_o, right, right_o, three, three_o, cots = r.need(0, 1, 2, 3, 4, 5, 6)
    half, hidden, width = r.kept[0].shape[0], right.shape[1], cots.shape[1]
    rows = right.shape[0]
    cot = cots.at[pl.ds(pl.multiple_of(core[0] * rows, rows), rows), :]
    cot_o = cots.at[pl.ds(pl.multiple_of((1 - core[0]) * rows, rows), rows), :]
    for place, of in ((0, 1 - bit[0]), (1, bit[0])):
        out = r.kept[place]

        def grads(at):
            rows = pl.ds(pl.multiple_of(of * half + at.start, min(half, TILE)), at.size)
            out[at, :hidden] = (dot_t(left[:, rows], right[...]) + dot_t(left_o[:, rows], right_o[...])).astype(BF)
            out[at, hidden : hidden + width] = (
                dot_t(three[:, rows], cot[...]) + dot_t(three_o[:, rows], cot_o[...])
            ).astype(BF)

        tiles(half, grads)
    feats, feats_o, back, back_o = r.need(7, 8, 9, 10)
    units = back.shape[1]
    for place, of in ((0, 1 - bit[0]), (1, bit[0])):
        out = r.kept[place]
        groups = feats.shape[1] // 2 // half
        for g in range(groups):
            lanes = slice(hidden + width + g * units, hidden + width + (g + 1) * units)

            def grads(at):
                rows = pl.ds(pl.multiple_of((of * groups + g) * half + at.start, min(half, TILE)), at.size)
                out[at, lanes] = (dot_t(feats[:, rows], back[...]) + dot_t(feats_o[:, rows], back_o[...])).astype(BF)

            tiles(half, grads)
        r.store(place)


def finish_kernel(factor, r, bit):
    (grad,) = r.kept
    parts = r.need(0, 1)
    half = parts[0].shape[0]
    step = min(half, 64)
    for part, of in zip(parts, (bit[0], 1 - bit[0])):

        def chunk(j, carry):
            at = pl.ds(pl.multiple_of(j * step, step), step)
            to = pl.ds(pl.multiple_of(of * half + j * step, step), step)
            grad[to, :] = part[at, :].astype(F32) * factor
            return carry

        lax.fori_loop(0, half // step, chunk, 0)


def finish_side_kernel(factor, r, bit):
    one, two, four = r.kept
    parts = r.need(0, 1)
    half = parts[0].shape[0]
    step = min(half, 64)
    hidden, width, units = two.shape[1], four.shape[1], one.shape[1]
    groups = one.shape[0] // 2 // half
    for part, of in zip(parts, (bit[0], 1 - bit[0])):

        def chunk(j, carry):
            at = pl.ds(pl.multiple_of(j * step, step), step)
            for g in range(groups):
                to = pl.ds(pl.multiple_of((of * groups + g) * half + j * step, step), step)
                lanes = slice(hidden + width + g * units, hidden + width + (g + 1) * units)
                one[to, :] = part[at, lanes].astype(F32) * factor
            return carry

        lax.fori_loop(0, half // step, chunk, 0)
    r.store(0)
    for part, of in zip(parts, (bit[0], 1 - bit[0])):

        def chunk(j, carry):
            at = pl.ds(pl.multiple_of(j * step, step), step)
            to = pl.ds(pl.multiple_of(of * half + j * step, step), step)
            two[to, :] = part[at, :hidden].astype(F32) * factor
            four[to, :] = part[at, hidden : hidden + width].astype(F32) * factor
            return carry

        lax.fori_loop(0, half // step, chunk, 0)


def pack_kernel(peers_of, r, place, counts, core):
    rows, cots = r.need(0, 1)
    (pack,) = r.kept
    slots, width = cots.shape[1:]
    span = slots // 2
    base = 1 << 7
    begin = pl.multiple_of(core[0] * span, span)
    slot = lax.broadcasted_iota(jnp.int32, (span, width), 0) + begin
    line = lax.broadcasted_iota(jnp.int32, (8, slots), 0)
    lane = lax.broadcasted_iota(jnp.int32, (8, slots), 1)
    peers = peers_of(place, core[0])
    pack[:, span:, :] = jnp.zeros((pack.shape[0], 8, width), BF)
    for k in range(pack.shape[0]):
        peer = peers(k)
        count = counts[peer]
        block = cots[peer, pl.ds(begin, span), :].astype(F32)
        pack[k, :span, :] = jnp.where(slot < count, block, 0.0).astype(BF)
        row = jnp.where(lane < count, jnp.broadcast_to(rows[pl.ds(peer, 1), :], line.shape), 0)
        digits = jnp.where(line == 0, row // base, jnp.where(line == 1, row % base, 0))
        pack[k, span:, :slots] = digits.astype(F32).astype(BF)


def hot_kernel(there, r, rows, core, rows_f32, cots):
    mine, other, _ = r.need(0, 1, 2)
    fetched, table = r.kept
    peers, span = fetched.shape[0], fetched.shape[1]
    begin = core[0] * span
    cots[core[0]] = mine[:, :span, :].astype(F32) * learn_rate
    cots[1 - core[0]] = other[:, :span, :].astype(F32) * learn_rate

    def fetch(k, carry):
        for j in range(span):
            rows_f32[k, pl.ds(j, 1), :] = table[pl.ds(rows[k * 2 * span + begin + j], 1), :]
        return carry

    lax.fori_loop(0, peers, fetch, 0)
    fetched[...] = rows_f32[...].astype(BF)
    r.store(0)

    for k in range(peers):
        own = jnp.where(core[0] == 0, k, there[k])
        for half, block in ((0, k), (1, there[k])):
            for j in range(span):
                at = pl.ds(rows[own * 2 * span + half * span + j], 1)
                table[at, :] = table[at, :] - cots[half, block, pl.ds(j, 1), :]


def unpack_kernel(peers_of, r, place, counts, core):
    mine, other = r.need(0, 1)
    (emb,) = r.kept
    span = mine.shape[1]
    line = lax.broadcasted_iota(jnp.int32, mine.shape[1:], 0)
    for source, half in ((mine, core[0]), (other, 1 - core[0])):
        peers = peers_of(place, half)
        for k in range(mine.shape[0]):
            peer = peers(k)
            count = counts[peer]
            begin = pl.multiple_of(half * span, span)
            block = jnp.where(line + begin < count, source[k].astype(F32), 0.0)
            emb[peer, pl.ds(begin, span), :] = block.astype(BF)


def swap(x):
    return lax.ppermute(x, "mp", [(0, 1), (1, 0)])


def in_order(mine, other, core, axis):
    first = jnp.where(core == 0, mine, other)
    second = jnp.where(core == 0, other, mine)
    return jnp.concatenate([first, second], axis=axis)


def as_rows(blocks, lanes):
    number, rows, width = blocks.shape
    across = lanes // width
    down = -(-number // across)
    blocks = jnp.pad(blocks, ((0, down * across - number), (0, 0), (0, 0)))
    return blocks.reshape(down, across, rows, width).transpose(0, 2, 1, 3).reshape(down * rows, lanes)


def as_blocks(rows, shape):
    number, height, width = shape
    across = rows.shape[1] // width
    blocks = rows.reshape(-1, height, across, width).transpose(0, 2, 1, 3)
    return blocks.reshape(-1, height, width)[:number]


def make_reduce(count, hops):
    steps = len(hops)

    def order_for(name):
        first, second, third = hops[:3]
        other = [second, first, third] if name == "three" else [third, first, second]
        return [hops, other + hops[3:]]

    def bit_of(name, s):
        order = order_for(name)
        core = lax.axis_index("mp")
        place = lax.axis_index("dp")
        dual = jnp.where(core == 0, order[0][s][1], order[1][s][1])
        return lax.population_count(place & dual) & 1

    def reduce(sent, kept, name, rider=None, turn=None, halvings=3):
        blocks = [rider]
        order = order_for(name)

        def exchange(x, s, kind):
            pairs = [
                (i * 2 + c, (i ^ order[c][s][0]) * 2 + c) for i in range(count) for c in range(2)
            ]
            rows = x.shape[0]
            if blocks[0] is None:
                return lax.ppermute(x, ("dp", "mp"), pairs)
            block = blocks[0].shape[1:]
            split = blocks[0].reshape((-1, 2, 1 << s) + block)
            leaving = split[:, 1].reshape((-1,) + block)
            x = leaving if kind == "home" else jnp.concatenate([x, as_rows(leaving, x.shape[1])], axis=0)
            came = lax.ppermute(x, ("dp", "mp"), pairs)
            joining = came if kind == "home" else as_blocks(came[rows:], leaving.shape)
            joining = joining.reshape(split[:, 1].shape)
            blocks[0] = jnp.stack([split[:, 0], joining], axis=1).reshape((-1,) + block)
            return came[:rows] if kind != "full" or s else came

        def bit(s):
            return bit_of(name, s)

        def total(terms, shift, size):
            return sum(lax.dynamic_slice_in_dim(t, at + shift, size, 0).astype(F32) for t, at in terms)

        terms = [(kept, 0), (exchange(sent, 0, "half"), 0)]
        size = kept.shape[0]
        for s in range(1, halvings):
            size //= 2
            b = bit(s)
            came = exchange(total(terms, (1 - b) * size, size).astype(BF), s, "half")
            terms = [(t, at + b * size) for t, at in terms] + [(came, 0)]
        mine = total(terms, 0, size).astype(BF)
        for s in range(halvings, steps):
            mine = (mine.astype(F32) + exchange(mine, s, "both").astype(F32)).astype(BF)
        if turn is not None:
            blocks[0] = turn(blocks[0])
            for s in range(halvings, steps):
                exchange(blocks[0], s, "home")
        for s in reversed(range(1, halvings)):
            came = exchange(mine, s, "full")
            b = bit(s)
            mine = jnp.concatenate([jnp.where(b == 0, mine, came), jnp.where(b == 0, came, mine)], axis=0)
        came = exchange(mine, 0, "full")
        return (mine, came), blocks[0]

    def combos_of(core):
        combos = [0]
        for mask, _ in order_for("three")[core]:
            combos += [c ^ mask for c in combos]
        return combos

    return reduce, bit_of, combos_of


def make_local(count, hops):
    reduce, bit_of, combos_of = make_reduce(count, hops)
    combos = [combos_of(0), combos_of(1)]
    there = [combos[1].index(c) for c in combos[0]]

    def local(
        hot_rows,
        hot_count,
        hot_cot,
        table,
        cold_ids,
        hash_mult,
        hash_add,
        layer_one,
        layer_two,
        layer_three,
        layer_four,
        cold_cot,
    ):
        core = lax.axis_index("mp")
        place = lax.axis_index("dp")
        width = table.shape[1]
        one_o, two_o, three_o, four_o = swap(layer_one), swap(layer_two), swap(layer_three), swap(layer_four)

        number = cold_ids.shape[0] // 2
        depth, half = layer_one.shape
        hidden = layer_two.shape[1]
        unit = 2 * number * half * depth
        feats, act_one_m, slope_one_m = call(
            first_kernel,
            [((number, depth), BF), ((number, half), BF), ((number, half), F32)],
            [cold_ids[:, None], hash_mult[None, :], hash_add[None, :], layer_one],
            scalars=[core],
            flops=unit * 2,
        )
        feats_p = swap(feats)
        act_one_o, slope_one_o, act_two, slope_two, emb, back_three_m, back_three_o, act_three_m, act_three_o = call(
            second_kernel,
            [
                ((number, half), BF), ((number, half), F32), ((number, hidden), BF), ((number, hidden), F32),
                ((number, width), BF), ((number, half), BF), ((number, half), BF), ((number, half), BF),
                ((number, half), BF),
            ],
            [feats, one_o, act_one_m, layer_two, two_o, layer_three, three_o, layer_four, four_o, cold_cot],
            [((number, half), F32)] * 2,
            scalars=[core],
            flops=unit * 6,
        )
        act_two_p, back_three_p = swap(act_two), swap(back_three_o)
        act_three_p, act_one_p = swap(act_three_o), swap(act_one_o)
        back_two, back_one_m, back_one_o = call(
            back_kernel,
            [((number, hidden), BF), ((number, half), BF), ((number, half), BF)],
            [
                back_three_m, back_three_o, layer_three, three_o, slope_two, two_o, slope_one_o, layer_two, slope_one_m,
            ],
            flops=unit * 4,
        )
        back_two_p, back_one_p = swap(back_two), swap(back_one_o)
        cold_emb = in_order(emb, swap(emb), core, 0)
        factor = float(cold_ids.shape[0] * count) ** (-0.5)
        slots = hot_rows.shape[2]
        span = slots // 2

        def peers_of(place, core):
            return lambda k: place[0] ^ jnp.where(core == 0, combos[0][k], combos[1][k])

        (pack,) = call(
            functools.partial(pack_kernel, peers_of),
            [((count, span + 8, width), BF)],
            [hot_rows[0], hot_cot[0]],
            scalars=[place, hot_count[0], core],
        )
        sent, kept = call(
            grad_kernel,
            [((hidden // 2, half), BF)] * 2,
            [act_two, act_two_p, back_three_m, back_three_p],
            scalars=[bit_of("three", 0)],
            flops=unit * 2,
        )
        updated = []

        def turn(pack):
            digits = pack[:, span : span + 2, :slots].astype(F32).astype(jnp.int32)
            wanted = (digits[:, 0] * 128 + digits[:, 1]).reshape(-1)
            other_pack = swap(pack)
            fetched, new_table = call(
                functools.partial(hot_kernel, there),
                [((count, span, width), BF), (table.shape, F32)],
                [pack, other_pack, table],
                [((count, span, width), F32), ((2, count, span, width), F32)],
                scalars=[wanted, core],
                shared=[(2, 1)],
            )
            updated.append(new_table)
            return fetched

        halves, returned = reduce(sent, kept, "three", pack, turn)
        (new_table,) = updated
        (grad_three,) = call(
            functools.partial(finish_kernel, factor), [((hidden, half), F32)], halves, scalars=[bit_of("three", 0)]
        )
        sent, kept = call(
            grads_kernel,
            [((half // 2, hidden + width + depth), BF)] * 2,
            [
                act_one_m, act_one_p, back_two, back_two_p, act_three_m, act_three_p, cold_cot,
                feats, feats_p, back_one_m, back_one_p,
            ],
            scalars=[bit_of("one", 0), core],
            flops=unit * 4,
        )
        halves, _ = reduce(sent, kept, "one")
        grad_one, grad_two, grad_four = call(
            functools.partial(finish_side_kernel, factor),
            [((depth, half), F32), ((half, hidden), F32), ((half, width), F32)],
            halves,
            scalars=[bit_of("one", 0)],
        )

        other_returned = swap(returned)
        (hot_emb,) = call(
            functools.partial(unpack_kernel, peers_of),
            [((count, slots, width), BF)],
            [returned, other_returned],
            scalars=[place, hot_count[0], core],
        )
        hot_emb = hot_emb[None]
        return hot_emb, new_table, cold_emb, grad_one, grad_two, grad_three, grad_four

    return local


def solution(mesh):
    in_specs = (
        P("dp", None, None),
        P("dp", None),
        P("dp", None, None, None),
        P("dp", None),
        P("dp"),
        P(),
        P(),
        P(None, "mp"),
        P("mp", None),
        P(None, "mp"),
        P("mp", None),
        P("dp", None),
    )
    out_specs = (
        P("dp", None, None, None),
        P("dp", None),
        P("dp", None),
        P(None, "mp"),
        P("mp", None),
        P(None, "mp"),
        P("mp", None),
    )
    local = make_local(mesh.shape["dp"], hops_of(mesh))

    return jax.shard_map(local, mesh=mesh, in_specs=in_specs, out_specs=out_specs, check_vma=False)
```

```python
import functools

import jax
import jax.numpy as jnp
from jax import lax
from jax.experimental import pallas as pl
from jax.experimental.pallas import tpu as pltpu
from jax.sharding import PartitionSpec as P


learn_rate = 0.5
modulus = 1000003
BF = jnp.bfloat16
F32 = jnp.float32


def hops_of(mesh):
    count = mesh.shape["dp"]
    coords = [getattr(d, "coords", None) for d in mesh.devices[:, 0]]
    sizes = None
    if all(c is not None for c in coords):
        sizes = [len({c[axis] for c in coords}) for axis in range(3)]
        if sizes[0] * sizes[1] * sizes[2] != count:
            sizes = None
    if sizes is None:
        sizes = [2] * (count.bit_length() - 1)
    hops, base = [], 0
    for size in sizes:
        bits = size.bit_length() - 1
        assert size == 1 << bits
        if bits == 2:
            hops.append([(1 << base, 3 << base), (3 << base, 2 << base)])
        elif bits:
            hops.append([(1 << (base + k), 1 << (base + k)) for k in range(bits)])
        base += bits
    assert 1 << base == count
    flat = []
    while any(hops):
        for group in hops:
            if group:
                flat.append(group.pop(0))
    return flat


TILE = 512


def dot(a, b):
    return jnp.dot(a, b, preferred_element_type=F32)


def dot_t(a, b):
    return lax.dot_general(a, b, (((0,), (0,)), ((), ())), preferred_element_type=F32)


def dot_bt(a, b):
    return lax.dot_general(a, b, (((1,), (1,)), ((), ())), preferred_element_type=F32)


def gates(value):
    sig = jax.nn.sigmoid(value)
    return (value * sig).astype(BF), sig * (1.0 + value * (1.0 - sig))


def tiles(size, body):
    step = min(size, TILE)

    def run(j, carry):
        body(pl.ds(pl.multiple_of(j * step, step), step))
        return carry

    lax.fori_loop(0, size // step, run, 0)


class Refs:
    def __init__(self, inputs, outputs, held, kept, load_sems, store_sems):
        self.held, self.kept = held, kept
        self.loads = [pltpu.make_async_copy(s, d, load_sems.at[i]) for i, (s, d) in enumerate(zip(inputs, held))]
        self.stores = [pltpu.make_async_copy(s, d, store_sems.at[i]) for i, (s, d) in enumerate(zip(kept, outputs))]
        self.outputs, self.sems = outputs, store_sems
        self.waited, self.put, self.started = set(), set(), []
        for load in self.loads:
            load.start()

    def need(self, *which):
        for i in which:
            if i not in self.waited:
                self.loads[i].wait()
                self.waited.add(i)
        return tuple(self.held[i] for i in which)

    def store(self, *which):
        for i in which:
            self.stores[i].start()
            self.put.add(i)
            self.started.append(self.stores[i])

    def store_rows(self, i, start, size, again):
        at = pl.ds(pl.multiple_of(start, size), size)
        sem = self.sems.at[i + again * len(self.stores)]
        copy = pltpu.make_async_copy(self.kept[i].at[at, :], self.outputs[i].at[at, :], sem)
        copy.start()
        self.put.add(i)
        self.started.append(copy)

    def finish(self):
        self.need(*range(len(self.loads)))
        self.store(*(i for i in range(len(self.stores)) if i not in self.put))
        for copy in self.started:
            copy.wait()


def call(kernel, outs, args, scratch=(), flops=0, scalars=(), shared=()):
    shapes = [jax.ShapeDtypeStruct(shape, kind) for shape, kind in outs]
    moved = sum(x.size * x.dtype.itemsize for x in list(args) + shapes)
    far = pl.BlockSpec(memory_space=pltpu.MemorySpace.HBM)
    near = pl.BlockSpec(memory_space=pltpu.SMEM)
    p, n, m = len(scalars), len(args), len(shapes)
    shared = dict(shared)
    alone = [i for i in range(n) if i not in shared]
    scalars = [jnp.asarray(x, jnp.int32).reshape(-1) for x in scalars]

    def body(*refs):
        numbers, refs = refs[:p], refs[p:]
        inputs, outputs, refs = refs[:n], refs[n : n + m], refs[n + m :]
        own, kept, rest = refs[: len(alone)], refs[len(alone) : len(alone) + m], refs[len(alone) + m :]
        own = dict(zip(alone, own))
        held = [own[i] if i in own else kept[shared[i]] for i in range(n)]
        r = Refs(inputs, outputs, held, kept, rest[-2], rest[-1])
        kernel(r, *numbers, *rest[:-2])
        r.finish()

    return pl.pallas_call(
        body,
        out_shape=shapes,
        in_specs=[near] * p + [far] * n,
        out_specs=[far] * m,
        scratch_shapes=[
            *(pltpu.VMEM(args[i].shape, args[i].dtype) for i in alone),
            *(pltpu.VMEM(x.shape, x.dtype) for x in shapes),
            *(pltpu.VMEM(shape, kind) for shape, kind in scratch),
            pltpu.SemaphoreType.DMA((n,)),
            pltpu.SemaphoreType.DMA((2 * m,)),
        ],
        cost_estimate=pl.CostEstimate(flops=flops, bytes_accessed=moved, transcendentals=0),
    )(*scalars, *args)


def first_kernel(r, core):
    ids, mult, add = r.need(0, 1, 2)
    feats, act, slope = r.kept
    rows = feats.shape[0]
    step = min(rows, 64)

    def hash_rows(j, carry):
        at = pl.ds(pl.multiple_of(j * step, step), step)
        own = pl.ds(pl.multiple_of(core[0] * rows + j * step, step), step)
        hashed = ids[own, :] * mult[...] + add[...]
        quotient = (hashed.astype(F32) * (1.0 / modulus)).astype(jnp.int32)
        left = hashed - quotient * modulus
        left = jnp.where(left < 0, left + modulus, left)
        left = jnp.where(left >= modulus, left - modulus, left)
        feats[at, :] = (left.astype(F32) * (2.0 / 1000002.0) - 1.0).astype(BF)
        return carry

    lax.fori_loop(0, rows // step, hash_rows, 0)
    r.store(0)
    (one,) = r.need(3)

    def layer(at):
        act[:, at], slope[:, at] = gates(dot(feats[...], one[:, at]))

    tiles(one.shape[1], layer)


def second_kernel(r, core, slope_three_m, slope_three_o):
    act_o, slope_one_o, act_two, slope_two, emb, back_m, back_o, act_three_m, act_three_o = r.kept
    feats, one_o = r.need(0, 1)

    def layer_one(at):
        act_o[:, at], slope_one_o[:, at] = gates(dot(feats[...], one_o[:, at]))

    tiles(one_o.shape[1], layer_one)
    r.store(0, 1)
    act_m, two_m, two_o = r.need(2, 3, 4)

    def layer_two(at):
        act_two[:, at], slope_two[:, at] = gates(
            dot(act_m[...], two_m[:, at]) + dot(act_o[...], two_o[:, at])
        )

    tiles(two_m.shape[1], layer_two)
    r.store(2, 3)
    three_m, three_o, four_m, four_o, cots = r.need(5, 6, 7, 8, 9)
    rows = act_two.shape[0]
    cot = cots.at[pl.ds(pl.multiple_of(core[0] * rows, rows), rows), :]
    for three, four, act, slope, back, places in (
        (three_o, four_o, act_three_o, slope_three_o, back_o, (8, 6)),
        (three_m, four_m, act_three_m, slope_three_m, back_m, (7, 5)),
    ):

        def layer_three(at):
            act[:, at], slope[:, at] = gates(dot(act_two[...], three[:, at]))
            back[:, at] = (dot_bt(cot[...], four[at, :]) * slope[:, at]).astype(BF)

        tiles(three.shape[1], layer_three)
        r.store(*places)
    emb[...] = (dot(act_three_m[...], four_m[...]) + dot(act_three_o[...], four_o[...])).astype(BF)


def back_kernel(r):
    back_two, back_one_m, back_one_o = r.kept
    back_m, back_o, three_m, three_o, slope_two = r.need(0, 1, 2, 3, 4)

    def go_back(at):
        back_two[:, at] = (
            (dot_bt(back_m[...], three_m[at, :]) + dot_bt(back_o[...], three_o[at, :])) * slope_two[:, at]
        ).astype(BF)

    tiles(three_m.shape[0], go_back)
    r.store(0)
    two_o, slope_o, two_m, slope_m = r.need(5, 6, 7, 8)
    for two, slope, back, place in ((two_o, slope_o, back_one_o, 2), (two_m, slope_m, back_one_m, 1)):

        def go_back(at):
            back[:, at] = (dot_bt(back_two[...], two[at, :]) * slope[:, at]).astype(BF)

        tiles(two.shape[0], go_back)
        r.store(place)


def grad_kernel(r, bit):
    left, left_o, right, right_o = r.need(0, 1, 2, 3)
    half = r.kept[0].shape[0]
    for place, of in ((0, 1 - bit[0]), (1, bit[0])):
        out = r.kept[place]

        def grads(at):
            rows = pl.ds(pl.multiple_of(of * half + at.start, min(half, TILE)), at.size)
            out[at, :] = (dot_t(left[:, rows], right[...]) + dot_t(left_o[:, rows], right_o[...])).astype(BF)

        tiles(half, grads)
        r.store(place)


def grads_kernel(r, bit, core):
    left, left_o, right, right_o, three, three_o, cots = r.need(0, 1, 2, 3, 4, 5, 6)
    half, hidden, width = r.kept[0].shape[0], right.shape[1], cots.shape[1]
    rows = right.shape[0]
    cot = cots.at[pl.ds(pl.multiple_of(core[0] * rows, rows), rows), :]
    cot_o = cots.at[pl.ds(pl.multiple_of((1 - core[0]) * rows, rows), rows), :]
    for place, of in ((0, 1 - bit[0]), (1, bit[0])):
        out = r.kept[place]

        def grads(at):
            rows = pl.ds(pl.multiple_of(of * half + at.start, min(half, TILE)), at.size)
            out[at, :hidden] = (dot_t(left[:, rows], right[...]) + dot_t(left_o[:, rows], right_o[...])).astype(BF)
            out[at, hidden : hidden + width] = (
                dot_t(three[:, rows], cot[...]) + dot_t(three_o[:, rows], cot_o[...])
            ).astype(BF)

        tiles(half, grads)
    feats, feats_o, back, back_o = r.need(7, 8, 9, 10)
    units = back.shape[1]
    for place, of in ((0, 1 - bit[0]), (1, bit[0])):
        out = r.kept[place]
        groups = feats.shape[1] // 2 // half
        for g in range(groups):
            lanes = slice(hidden + width + g * units, hidden + width + (g + 1) * units)

            def grads(at):
                rows = pl.ds(pl.multiple_of((of * groups + g) * half + at.start, min(half, TILE)), at.size)
                out[at, lanes] = (dot_t(feats[:, rows], back[...]) + dot_t(feats_o[:, rows], back_o[...])).astype(BF)

            tiles(half, grads)
        r.store(place)


def finish_kernel(factor, r, bit):
    (grad,) = r.kept
    parts = r.need(0, 1)
    half = parts[0].shape[0]
    step = min(half, 64)
    for part, of in zip(parts, (bit[0], 1 - bit[0])):

        def chunk(j, carry):
            at = pl.ds(pl.multiple_of(j * step, step), step)
            to = pl.ds(pl.multiple_of(of * half + j * step, step), step)
            grad[to, :] = part[at, :].astype(F32) * factor
            return carry

        lax.fori_loop(0, half // step, chunk, 0)


def finish_side_kernel(factor, r, bit):
    one, two, four = r.kept
    half = r.held[0].shape[0]
    step = min(half, 64)
    hidden, width, units = two.shape[1], four.shape[1], one.shape[1]
    groups = one.shape[0] // 2 // half
    for again, of in enumerate((bit[0], 1 - bit[0])):
        (part,) = r.need(again)

        def chunk(j, carry):
            at = pl.ds(pl.multiple_of(j * step, step), step)
            for g in range(groups):
                to = pl.ds(pl.multiple_of((of * groups + g) * half + j * step, step), step)
                lanes = slice(hidden + width + g * units, hidden + width + (g + 1) * units)
                one[to, :] = part[at, lanes].astype(F32) * factor
            return carry

        lax.fori_loop(0, half // step, chunk, 0)
        r.store_rows(0, of * groups * half, groups * half, again)

        def chunk(j, carry):
            at = pl.ds(pl.multiple_of(j * step, step), step)
            to = pl.ds(pl.multiple_of(of * half + j * step, step), step)
            two[to, :] = part[at, :hidden].astype(F32) * factor
            four[to, :] = part[at, hidden : hidden + width].astype(F32) * factor
            return carry

        lax.fori_loop(0, half // step, chunk, 0)
        r.store_rows(1, of * half, half, again)
        r.store_rows(2, of * half, half, again)


def pack_kernel(peers_of, r, place, counts, core):
    rows, cots = r.need(0, 1)
    (pack,) = r.kept
    slots, width = cots.shape[1:]
    span = slots // 2
    base = 1 << 7
    begin = pl.multiple_of(core[0] * span, span)
    slot = lax.broadcasted_iota(jnp.int32, (span, width), 0) + begin
    line = lax.broadcasted_iota(jnp.int32, (8, slots), 0)
    lane = lax.broadcasted_iota(jnp.int32, (8, slots), 1)
    peers = peers_of(place, core[0])
    pack[:, span:, :] = jnp.zeros((pack.shape[0], 8, width), BF)
    for k in range(pack.shape[0]):
        peer = peers(k)
        count = counts[peer]
        block = cots[peer, pl.ds(begin, span), :].astype(F32)
        pack[k, :span, :] = jnp.where(slot < count, block, 0.0).astype(BF)
        row = jnp.where(lane < count, jnp.broadcast_to(rows[pl.ds(peer, 1), :], line.shape), 0)
        digits = jnp.where(line == 0, row // base, jnp.where(line == 1, row % base, 0))
        pack[k, span:, :slots] = digits.astype(F32).astype(BF)


def hot_kernel(there, r, rows, core, rows_f32, cots):
    mine, other, _ = r.need(0, 1, 2)
    fetched, table = r.kept
    peers, span = fetched.shape[0], fetched.shape[1]
    begin = core[0] * span
    cots[core[0]] = mine[:, :span, :].astype(F32) * learn_rate
    cots[1 - core[0]] = other[:, :span, :].astype(F32) * learn_rate

    def fetch(k, carry):
        for j in range(span):
            rows_f32[k, pl.ds(j, 1), :] = table[pl.ds(rows[k * 2 * span + begin + j], 1), :]
        return carry

    lax.fori_loop(0, peers, fetch, 0)
    fetched[...] = rows_f32[...].astype(BF)
    r.store(0)

    for k in range(peers):
        own = jnp.where(core[0] == 0, k, there[k])
        for half, block in ((0, k), (1, there[k])):
            for j in range(span):
                at = pl.ds(rows[own * 2 * span + half * span + j], 1)
                table[at, :] = table[at, :] - cots[half, block, pl.ds(j, 1), :]


def unpack_kernel(peers_of, r, place, counts, core):
    mine, other = r.need(0, 1)
    (emb,) = r.kept
    span = mine.shape[1]
    line = lax.broadcasted_iota(jnp.int32, mine.shape[1:], 0)
    for source, half in ((mine, core[0]), (other, 1 - core[0])):
        peers = peers_of(place, half)
        for k in range(mine.shape[0]):
            peer = peers(k)
            count = counts[peer]
            begin = pl.multiple_of(half * span, span)
            block = jnp.where(line + begin < count, source[k].astype(F32), 0.0)
            emb[peer, pl.ds(begin, span), :] = block.astype(BF)


def swap(x):
    return lax.ppermute(x, "mp", [(0, 1), (1, 0)])


def in_order(mine, other, core, axis):
    first = jnp.where(core == 0, mine, other)
    second = jnp.where(core == 0, other, mine)
    return jnp.concatenate([first, second], axis=axis)


def as_rows(blocks, lanes):
    number, rows, width = blocks.shape
    across = lanes // width
    down = -(-number // across)
    blocks = jnp.pad(blocks, ((0, down * across - number), (0, 0), (0, 0)))
    return blocks.reshape(down, across, rows, width).transpose(0, 2, 1, 3).reshape(down * rows, lanes)


def as_blocks(rows, shape):
    number, height, width = shape
    across = rows.shape[1] // width
    blocks = rows.reshape(-1, height, across, width).transpose(0, 2, 1, 3)
    return blocks.reshape(-1, height, width)[:number]


def make_reduce(count, hops):
    steps = len(hops)

    def order_for(name):
        first, second, third = hops[:3]
        other = [second, first, third] if name == "three" else [third, first, second]
        return [hops, other + hops[3:]]

    def bit_of(name, s):
        order = order_for(name)
        core = lax.axis_index("mp")
        place = lax.axis_index("dp")
        dual = jnp.where(core == 0, order[0][s][1], order[1][s][1])
        return lax.population_count(place & dual) & 1

    def reduce(sent, kept, name, rider=None, turn=None, halvings=3):
        blocks = [rider]
        order = order_for(name)

        def exchange(x, s, kind):
            pairs = [
                (i * 2 + c, (i ^ order[c][s][0]) * 2 + c) for i in range(count) for c in range(2)
            ]
            rows = x.shape[0]
            if blocks[0] is None:
                return lax.ppermute(x, ("dp", "mp"), pairs)
            block = blocks[0].shape[1:]
            split = blocks[0].reshape((-1, 2, 1 << s) + block)
            leaving = split[:, 1].reshape((-1,) + block)
            x = leaving if kind == "home" else jnp.concatenate([x, as_rows(leaving, x.shape[1])], axis=0)
            came = lax.ppermute(x, ("dp", "mp"), pairs)
            joining = came if kind == "home" else as_blocks(came[rows:], leaving.shape)
            joining = joining.reshape(split[:, 1].shape)
            blocks[0] = jnp.stack([split[:, 0], joining], axis=1).reshape((-1,) + block)
            return came[:rows] if kind != "full" or s else came

        def bit(s):
            return bit_of(name, s)

        def total(terms, shift, size):
            return sum(lax.dynamic_slice_in_dim(t, at + shift, size, 0).astype(F32) for t, at in terms)

        terms = [(kept, 0), (exchange(sent, 0, "half"), 0)]
        size = kept.shape[0]
        for s in range(1, halvings):
            size //= 2
            b = bit(s)
            came = exchange(total(terms, (1 - b) * size, size).astype(BF), s, "half")
            terms = [(t, at + b * size) for t, at in terms] + [(came, 0)]
        mine = total(terms, 0, size).astype(BF)
        for s in range(halvings, steps):
            mine = (mine.astype(F32) + exchange(mine, s, "both").astype(F32)).astype(BF)
        if turn is not None:
            blocks[0] = turn(blocks[0])
            for s in range(halvings, steps):
                exchange(blocks[0], s, "home")
        for s in reversed(range(1, halvings)):
            came = exchange(mine, s, "full")
            b = bit(s)
            mine = jnp.concatenate([jnp.where(b == 0, mine, came), jnp.where(b == 0, came, mine)], axis=0)
        came = exchange(mine, 0, "full")
        return (mine, came), blocks[0]

    def combos_of(core):
        combos = [0]
        for mask, _ in order_for("three")[core]:
            combos += [c ^ mask for c in combos]
        return combos

    return reduce, bit_of, combos_of


def make_local(count, hops):
    reduce, bit_of, combos_of = make_reduce(count, hops)
    combos = [combos_of(0), combos_of(1)]
    there = [combos[1].index(c) for c in combos[0]]

    def local(
        hot_rows,
        hot_count,
        hot_cot,
        table,
        cold_ids,
        hash_mult,
        hash_add,
        layer_one,
        layer_two,
        layer_three,
        layer_four,
        cold_cot,
    ):
        core = lax.axis_index("mp")
        place = lax.axis_index("dp")
        width = table.shape[1]
        one_o, two_o, three_o, four_o = swap(layer_one), swap(layer_two), swap(layer_three), swap(layer_four)

        number = cold_ids.shape[0] // 2
        depth, half = layer_one.shape
        hidden = layer_two.shape[1]
        unit = 2 * number * half * depth
        feats, act_one_m, slope_one_m = call(
            first_kernel,
            [((number, depth), BF), ((number, half), BF), ((number, half), F32)],
            [cold_ids[:, None], hash_mult[None, :], hash_add[None, :], layer_one],
            scalars=[core],
            flops=unit * 2,
        )
        feats_p = swap(feats)
        act_one_o, slope_one_o, act_two, slope_two, emb, back_three_m, back_three_o, act_three_m, act_three_o = call(
            second_kernel,
            [
                ((number, half), BF), ((number, half), F32), ((number, hidden), BF), ((number, hidden), F32),
                ((number, width), BF), ((number, half), BF), ((number, half), BF), ((number, half), BF),
                ((number, half), BF),
            ],
            [feats, one_o, act_one_m, layer_two, two_o, layer_three, three_o, layer_four, four_o, cold_cot],
            [((number, half), F32)] * 2,
            scalars=[core],
            flops=unit * 6,
        )
        act_two_p, back_three_p = swap(act_two), swap(back_three_o)
        act_three_p, act_one_p = swap(act_three_o), swap(act_one_o)
        back_two, back_one_m, back_one_o = call(
            back_kernel,
            [((number, hidden), BF), ((number, half), BF), ((number, half), BF)],
            [
                back_three_m, back_three_o, layer_three, three_o, slope_two, two_o, slope_one_o, layer_two, slope_one_m,
            ],
            flops=unit * 4,
        )
        back_two_p, back_one_p = swap(back_two), swap(back_one_o)
        cold_emb = in_order(emb, swap(emb), core, 0)
        factor = float(cold_ids.shape[0] * count) ** (-0.5)
        slots = hot_rows.shape[2]
        span = slots // 2

        def peers_of(place, core):
            return lambda k: place[0] ^ jnp.where(core == 0, combos[0][k], combos[1][k])

        (pack,) = call(
            functools.partial(pack_kernel, peers_of),
            [((count, span + 8, width), BF)],
            [hot_rows[0], hot_cot[0]],
            scalars=[place, hot_count[0], core],
        )
        sent, kept = call(
            grad_kernel,
            [((hidden // 2, half), BF)] * 2,
            [act_two, act_two_p, back_three_m, back_three_p],
            scalars=[bit_of("three", 0)],
            flops=unit * 2,
        )
        updated = []

        def turn(pack):
            digits = pack[:, span : span + 2, :slots].astype(F32).astype(jnp.int32)
            wanted = (digits[:, 0] * 128 + digits[:, 1]).reshape(-1)
            other_pack = swap(pack)
            fetched, new_table = call(
                functools.partial(hot_kernel, there),
                [((count, span, width), BF), (table.shape, F32)],
                [pack, other_pack, table],
                [((count, span, width), F32), ((2, count, span, width), F32)],
                scalars=[wanted, core],
                shared=[(2, 1)],
            )
            updated.append(new_table)
            return fetched

        halves, returned = reduce(sent, kept, "three", pack, turn)
        (new_table,) = updated
        (grad_three,) = call(
            functools.partial(finish_kernel, factor), [((hidden, half), F32)], halves, scalars=[bit_of("three", 0)]
        )
        sent, kept = call(
            grads_kernel,
            [((half // 2, hidden + width + depth), BF)] * 2,
            [
                act_one_m, act_one_p, back_two, back_two_p, act_three_m, act_three_p, cold_cot,
                feats, feats_p, back_one_m, back_one_p,
            ],
            scalars=[bit_of("one", 0), core],
            flops=unit * 4,
        )
        halves, _ = reduce(sent, kept, "one")
        grad_one, grad_two, grad_four = call(
            functools.partial(finish_side_kernel, factor),
            [((depth, half), F32), ((half, hidden), F32), ((half, width), F32)],
            halves,
            scalars=[bit_of("one", 0)],
        )

        other_returned = swap(returned)
        (hot_emb,) = call(
            functools.partial(unpack_kernel, peers_of),
            [((count, slots, width), BF)],
            [returned, other_returned],
            scalars=[place, hot_count[0], core],
        )
        hot_emb = hot_emb[None]
        return hot_emb, new_table, cold_emb, grad_one, grad_two, grad_three, grad_four

    return local


def solution(mesh):
    in_specs = (
        P("dp", None, None),
        P("dp", None),
        P("dp", None, None, None),
        P("dp", None),
        P("dp"),
        P(),
        P(),
        P(None, "mp"),
        P("mp", None),
        P(None, "mp"),
        P("mp", None),
        P("dp", None),
    )
    out_specs = (
        P("dp", None, None, None),
        P("dp", None),
        P("dp", None),
        P(None, "mp"),
        P("mp", None),
        P(None, "mp"),
        P("mp", None),
    )
    local = make_local(mesh.shape["dp"], hops_of(mesh))

    return jax.shard_map(local, mesh=mesh, in_specs=in_specs, out_specs=out_specs, check_vma=False)
```
